32 devices in a mesh: rows: 8 (over z, x), samp: 4 (over y, core).
Axes of the slice: x: 2, y: 2, z: 4, core: 2. Of those that a mesh axis runs over, the one named last changes fastest.
Arguments:
- noise: bfloat16 [6, 64, 512, 128], P(None, 'rows', 'samp'), may hold values from -6 to 6
- diag_inverse: bfloat16 [6, 64, 128, 128], P(None, 'rows'), may hold values from -0.5 to 0.5
- coupling: bfloat16 [5, 64, 16, 128, 128], P(None, 'rows'), may hold values from -0.125 to 0.125
- pattern: int32 [5, 64, 16], P(None, 'rows'), may hold values from 0 to 319, as said below
Outputs:
- samples: bfloat16 [6, 64, 512, 128], P(None, 'rows', 'samp')
- variance: float32 [6, 64, 128], P(None, 'rows')
The draws below stay inside these ranges and needn't reach their ends.
Inputs may be any that keep to these rules, and one draw needn't show every extreme that they name: pattern[l, s, k] names a block row of a level before l + 1; the entry k = 0 lies in level l; entries may repeat. Block rows s with equal s // 8 together name, within any one level, at most one of the block rows t that share one value of t // 8.
All inputs are finite; a program needn't handle non-finite values.
Results may differ from the reference program's by a relative error of at most 0.008.
Values may be sent and summed in bfloat16 or wider, within the bound.
A program may use at most 192 MiB of HBM per device.

```python
import jax
import jax.numpy as jnp

B = 128
LEVELS = 6
K = 16
SLOT_DEV = 8
SLOTS = 64
S = 512


def draw_pattern(key, part):
    table_key, level_key, device_key = jax.random.split(key, 3)
    device_count = SLOTS // SLOT_DEV
    table = jax.random.randint(table_key, (device_count, LEVELS - 1, device_count), 0, SLOT_DEV)
    level_ids = jnp.arange(LEVELS - 1, dtype=jnp.int32)[:, None, None]
    drawn = jax.random.randint(level_key, (LEVELS - 1, SLOTS, K), 0, level_ids + 1)
    first = jnp.broadcast_to(level_ids, (LEVELS - 1, SLOTS, 1))
    source = jnp.concatenate([first, drawn[:, :, 1:]], axis=2).astype(jnp.int32)
    device_ids = jax.random.randint(device_key, (LEVELS - 1, SLOTS, K), 0, device_count)
    owner = (jnp.arange(SLOTS, dtype=jnp.int32) // SLOT_DEV)[None, :, None]
    flat = (owner * (LEVELS - 1) + source) * device_count + device_ids
    chosen = jnp.take(table.reshape(-1), flat)
    return (source * SLOTS + device_ids * SLOT_DEV + chosen).astype(jnp.int32)


def levels(rng, shape, pieces, low, largest):
    def one(dim, shards_of):
        steps = jax.random.uniform(jax.random.fold_in(jax.random.fold_in(rng, 6), dim), (shards_of,), jnp.float32, low / len(pieces), largest / len(pieces))
        return jnp.repeat(jnp.exp(steps), shape[dim] // shards_of).reshape((-1,) + (1,) * (len(shape) - dim - 1))

    level = one(*pieces[0])
    for cut in pieces[1:]:
        level = level * one(*cut)
    return level


def centred(key, shape, scale, limit, pieces=(), kind=jnp.bfloat16):
    result = jax.random.normal(key, shape, jnp.float32) * scale
    if len(pieces) > 0:
        result = levels(key, shape, pieces, -0.22, 0.18) * result
    return jnp.clip(result, min=-limit, max=limit).astype(kind)


def setup_inputs(seed: int = 0) -> dict:
    arg_keys = jax.random.split(jax.random.key(seed), 5)
    return {
        "noise": centred(arg_keys[0], (LEVELS, SLOTS, S, B), 1.0, 6.0, ((1, 8), (2, 4))),
        "diag_inverse": centred(arg_keys[1], (LEVELS, SLOTS, B, B), B ** -0.5, 0.5, ((1, 8),)),
        "coupling": centred(arg_keys[2], (LEVELS - 1, SLOTS, K, B, B), (B * K) ** -0.5, 0.125, ((1, 8),)),
        "pattern": draw_pattern(jax.random.fold_in(arg_keys[4], 71), 0),
    }


def reference(noise, diag_inverse, coupling, pattern):
    solved = []
    for level_index in range(LEVELS):
        if level_index == 0:
            residual = noise[0].astype(jnp.float32)
        else:
            solved_rows = jnp.concatenate(solved, axis=0)
            picked = jnp.take(solved_rows, pattern[level_index - 1].astype(jnp.int32), axis=0)
            update = jnp.einsum("pksb,pkbc->psc", picked.astype(jnp.float32), coupling[level_index - 1].astype(jnp.float32))
            residual = noise[level_index].astype(jnp.float32) - update
        rounded = residual.astype(jnp.bfloat16)
        block = jnp.einsum("psb,pbc->psc", rounded.astype(jnp.float32), diag_inverse[level_index].astype(jnp.float32))
        solved.append(block.astype(jnp.bfloat16))
    samples = jnp.stack(solved, axis=0)
    wide = samples.astype(jnp.float32)
    variance = jnp.mean(wide * wide, axis=2)
    return samples, variance
```

```python
import functools

import jax
import jax.numpy as jnp
from jax import lax
from jax.experimental import pallas as pl
from jax.experimental.pallas import tpu as pltpu
from jax.sharding import PartitionSpec as P

MESH = pl.DeviceIdType.MESH
F32 = jnp.float32
BF16 = jnp.bfloat16


def farthest_first(n):
    return sorted(range(1, n), key=lambda o: -min(o, n - o))


def kernel(
    n, m, pat_ref, patv_ref, noise_hbm, diag_hbm, coup_hbm,
    samples_hbm, var_ref,
    noise, diag, coup, own, table, send, recv, need, want_v, want, sums, vrecv,
    noise_sem, diag_sem, coup_sem, out_sem, send_sem, recv_sem,
    nsend_sem, nrecv_sem, want_sem, vsend_sem, vrecv_sem,
):
    levels, slot_dev, samp, b = noise.shape
    fan = pat_ref.shape[2]
    me = lax.axis_index("rows")
    q = lax.axis_index("samp")
    order = farthest_first(n)

    def fetch(src, dst, sem, i):
        return pltpu.make_async_copy(src.at[i], dst.at[i], sem.at[i])

    for i in range(levels):
        fetch(noise_hbm, noise, noise_sem, i).start()
        fetch(diag_hbm, diag, diag_sem, i).start()
        if i > 0:
            fetch(coup_hbm, coup, coup_sem, i - 1).start()

    barrier = pltpu.get_barrier_semaphore()
    for o in range(1, n):
        pl.semaphore_signal(
            barrier, inc=1, device_id={"rows": lax.rem(me + o, n)}, device_id_type=MESH
        )
    for o in range(1, m):
        pl.semaphore_signal(
            barrier, inc=1, device_id={"samp": lax.rem(q + o, m)}, device_id_type=MESH
        )

    shape = (need.shape[0], need.shape[1], patv_ref.shape[1])
    dev = lax.broadcasted_iota(jnp.int32, shape, 0)
    lev = lax.broadcasted_iota(jnp.int32, shape, 1)
    key = lev * n + dev
    best = jnp.zeros(shape, jnp.int32)
    for t in range(levels - 1):
        entry = patv_ref[t : t + 1, :].reshape(1, 1, -1)
        holder = lax.div(entry, jnp.int32(slot_dev))
        slot = entry - holder * slot_dev
        best = jnp.maximum(best, jnp.where(holder == key, slot, 0))
    best = jnp.max(best, axis=2, keepdims=True)
    need[...] = jnp.broadcast_to(best, need.shape)
    want_v[0] = need[me]

    pl.semaphore_wait(barrier, n - 1 + m - 1)

    def need_copy(o):
        return pltpu.make_async_remote_copy(
            src_ref=need.at[lax.rem(me + o, n)],
            dst_ref=want_v.at[o],
            send_sem=nsend_sem.at[o],
            recv_sem=nrecv_sem.at[o],
            device_id={"rows": lax.rem(me + o, n)},
            device_id_type=MESH,
        )

    for o in order:
        need_copy(o).start()

    def block_copy(level, o):
        return pltpu.make_async_remote_copy(
            src_ref=send.at[level, o],
            dst_ref=recv.at[level, o],
            send_sem=send_sem.at[level, o],
            recv_sem=recv_sem.at[level, o],
            device_id={"rows": lax.rem(me + o, n)},
            device_id_type=MESH,
        )

    def finish(level, s, residual):
        x = jnp.dot(
            residual.astype(BF16), diag[level, s], preferred_element_type=F32
        ).astype(BF16)
        own[level, s] = x
        wide = x.astype(F32)
        sums[level, pl.ds(s, 1), :] = jnp.sum(wide * wide, axis=0, keepdims=True)

    def update(level, s):
        total = None
        for k in range(0, fan, 2):
            picked = [
                table[lax.div(pat_ref[level - 1, s, k + j], jnp.int32(slot_dev))]
                for j in range(2)
            ]
            part = jnp.dot(
                jnp.concatenate(picked, axis=1),
                coup[level - 1, s, pl.ds(k * b, 2 * b), :],
                preferred_element_type=F32,
            )
            total = part if total is None else total + part
        return total

    for level in range(levels):
        fetch(noise_hbm, noise, noise_sem, level).wait()
        fetch(diag_hbm, diag, diag_sem, level).wait()
        if level > 0:
            fetch(coup_hbm, coup, coup_sem, level - 1).wait()

        def row(s, carry, level=level):
            residual = noise[level, s].astype(F32)
            if level > 0:
                residual = residual - update(level, s)
            finish(level, s, residual)
            return carry

        lax.fori_loop(0, slot_dev, row, 0, unroll=2)

        if level == 0:
            for o in order:
                need_copy(o).wait()
            copy = pltpu.make_async_copy(want_v, want, want_sem)
            copy.start()
            copy.wait()

        if level < levels - 1:
            for o in order:
                send[level, o] = own[level, want[n - o, level, 0]]
                block_copy(level, o).start()
            table[level * n + me] = own[level, want[0, level, 0]]
        pltpu.make_async_copy(own.at[level], samples_hbm.at[level], out_sem.at[level]).start()
        if level < levels - 1:
            for o in reversed(order):
                block_copy(level, o).wait()
                table[level * n + lax.rem(me - o + n, n)] = recv[level, o]

    def var_copy(o):
        return pltpu.make_async_remote_copy(
            src_ref=sums,
            dst_ref=vrecv.at[o],
            send_sem=vsend_sem.at[o],
            recv_sem=vrecv_sem.at[o],
            device_id={"samp": lax.rem(q + o, m)},
            device_id_type=MESH,
        )

    for o in range(1, m):
        var_copy(o).start()
    vrecv[0] = sums[...]
    for o in range(1, m):
        var_copy(o).wait()
    total = vrecv[q]
    for j in range(1, m):
        total = total + vrecv[lax.rem(q - j + m, m)]
    var_ref[...] = total * (1.0 / (samp * m))
    for level in range(levels):
        pltpu.make_async_copy(own.at[level], samples_hbm.at[level], out_sem.at[level]).wait()


def body(n, m, noise, diag, coupling, pattern):
    levels, slot_dev, samp, b = noise.shape
    fan = coupling.shape[2]
    lead = -(-levels // 8) * 8
    any_spec = pl.BlockSpec(memory_space=pl.ANY)
    vmem_spec = pl.BlockSpec(memory_space=pltpu.VMEM)
    dma = pltpu.SemaphoreType.DMA
    coupling = coupling.reshape(levels - 1, slot_dev, fan * b, b)
    return pl.pallas_call(
        functools.partial(kernel, n, m),
        out_shape=(
            jax.ShapeDtypeStruct(noise.shape, BF16),
            jax.ShapeDtypeStruct((levels, slot_dev, b), F32),
        ),
        in_specs=[pl.BlockSpec(memory_space=pltpu.SMEM), vmem_spec, any_spec, any_spec, any_spec],
        out_specs=(any_spec, vmem_spec),
        scratch_shapes=[
            pltpu.VMEM(noise.shape, BF16),
            pltpu.VMEM(diag.shape, BF16),
            pltpu.VMEM(coupling.shape, BF16),
            pltpu.VMEM(noise.shape, BF16),
            pltpu.VMEM(((levels - 1) * n, samp, b), BF16),
            pltpu.VMEM((levels - 1, n, samp, b), BF16),
            pltpu.VMEM((levels - 1, n, samp, b), BF16),
            pltpu.VMEM((n, lead, 128), jnp.int32),
            pltpu.VMEM((n, lead, 128), jnp.int32),
            pltpu.SMEM((n, lead, 128), jnp.int32),
            pltpu.VMEM((levels, slot_dev, b), F32),
            pltpu.VMEM((m, levels, slot_dev, b), F32),
            dma((levels,)),
            dma((levels,)),
            dma((levels - 1,)),
            dma((levels,)),
            dma((levels - 1, n)),
            dma((levels - 1, n)),
            dma((n,)),
            dma((n,)),
            dma,
            dma((m,)),
            dma((m,)),
        ],
        compiler_params=pltpu.CompilerParams(
            collective_id=0, has_side_effects=True, vmem_limit_bytes=56 * 1024 * 1024
        ),
    )(pattern, pattern.reshape(levels - 1, slot_dev * fan), noise, diag, coupling)


def solution(mesh):
    placed = (
        P(None, "rows", "samp", None),
        P(None, "rows", None, None),
        P(None, "rows", None, None, None),
        P(None, "rows", None),
    )
    return jax.shard_map(
        functools.partial(body, mesh.shape["rows"], mesh.shape["samp"]),
        mesh=mesh,
        in_specs=placed,
        out_specs=(P(None, "rows", "samp", None), P(None, "rows", None)),
        check_vma=False,
    )
```

```python
import functools

import jax
import jax.numpy as jnp
from jax import lax
from jax.experimental import pallas as pl
from jax.experimental.pallas import tpu as pltpu
from jax.sharding import PartitionSpec as P

MESH = pl.DeviceIdType.MESH
F32 = jnp.float32
BF16 = jnp.bfloat16


GROUP = 4


def kernel(
    n, m, pat_ref, patv_ref, noise_hbm, diag_hbm, coup_hbm,
    samples_hbm, var_ref,
    noise, diag, coup, own, table, send, recv, need, want_v, want, sums, vrecv,
    noise_sem, diag_sem, coup_sem, out_sem, send_sem, recv_sem,
    nsend_sem, nrecv_sem, want_sem, vsend_sem, vrecv_sem,
):
    levels, slot_dev, samp, b = noise.shape
    fan = pat_ref.shape[2]
    me = lax.axis_index("rows")
    q = lax.axis_index("samp")
    half = samp // 2

    def fetch(src, dst, sem, i):
        return pltpu.make_async_copy(src.at[i], dst.at[i], sem.at[i])

    for i in range(levels):
        fetch(noise_hbm, noise, noise_sem, i).start()
        fetch(diag_hbm, diag, diag_sem, i).start()
    for i in range(levels - 1):
        fetch(coup_hbm, coup, coup_sem, i).start()

    barrier = pltpu.get_barrier_semaphore()
    for o in range(1, n):
        pl.semaphore_signal(
            barrier, inc=1, device_id={"rows": lax.rem(me + o, n)}, device_id_type=MESH
        )
    for o in range(1, m):
        pl.semaphore_signal(
            barrier, inc=1, device_id={"samp": lax.rem(q + o, m)}, device_id_type=MESH
        )

    shape = (need.shape[0], need.shape[1], fan)
    dev = lax.broadcasted_iota(jnp.int32, shape, 0)
    lev = lax.broadcasted_iota(jnp.int32, shape, 1)
    key = lev * n + dev
    best = jnp.zeros(shape, jnp.int32)
    for t in range(levels - 1):
        for s in range(slot_dev):
            entry = patv_ref[t, s : s + 1, :].reshape(1, 1, fan)
            holder = lax.div(entry, jnp.int32(slot_dev))
            slot = entry - holder * slot_dev
            best = jnp.maximum(best, jnp.where(holder == key, slot, 0))
    best = jnp.max(best, axis=2, keepdims=True)
    need[...] = jnp.broadcast_to(best, need.shape)
    want_v[0] = need[me]

    def need_copy(o):
        return pltpu.make_async_remote_copy(
            src_ref=need.at[lax.rem(me + o, n)],
            dst_ref=want_v.at[o],
            send_sem=nsend_sem.at[o],
            recv_sem=nrecv_sem.at[o],
            device_id={"rows": lax.rem(me + o, n)},
            device_id_type=MESH,
        )

    def block_copy(level, h, o):
        return pltpu.make_async_remote_copy(
            src_ref=send.at[level, h, o],
            dst_ref=recv.at[level, h, o],
            send_sem=send_sem.at[level, h, o],
            recv_sem=recv_sem.at[level, h, o],
            device_id={"rows": lax.rem(me + o, n)},
            device_id_type=MESH,
        )

    def holder_of(level, s, k):
        return lax.div(pat_ref[level - 1, s, k], jnp.int32(slot_dev))

    def solve(level, s, halves):
        low, count = halves[0] * half, len(halves) * half
        residual = noise[level, s, pl.ds(low, count), :].astype(F32)
        if level > 0:
            total = None
            for k in range(0, fan, 2):
                picked = [
                    jnp.concatenate(
                        [table[h, holder_of(level, s, k + j)] for h in halves], axis=0
                    )
                    for j in range(2)
                ]
                part = jnp.dot(
                    jnp.concatenate(picked, axis=1),
                    coup[level - 1, s, pl.ds(k * b, 2 * b), :],
                    preferred_element_type=F32,
                )
                total = part if total is None else total + part
            residual = residual - total
        return jnp.dot(
            residual.astype(BF16), diag[level, s], preferred_element_type=F32
        ).astype(BF16)

    def own_rows(level, halves):
        low, count = halves[0] * half, len(halves) * half

        def row(s, carry):
            x = solve(level, s, halves)
            own[level, s, pl.ds(low, count), :] = x
            wide = x.astype(F32)
            part = jnp.sum(wide * wide, axis=0, keepdims=True)
            if low > 0:
                part = part + sums[level, pl.ds(s, 1), :]
            sums[level, pl.ds(s, 1), :] = part
            return carry

        lax.fori_loop(0, slot_dev, row, 0, unroll=8)

    def keep_own(level):
        mine = own[level, want[0, level, 0]]
        for h in range(2):
            table[h, level * n + me] = mine[h * half : (h + 1) * half]

    def receive(level, h):
        for o in range(1, n):
            block_copy(level, h, o).wait()
            table[h, level * n + lax.rem(me - o + n, n)] = recv[level, h, o]

    def write_out(level):
        return pltpu.make_async_copy(own.at[level], samples_hbm.at[level], out_sem.at[level])

    def loaded(level):
        fetch(noise_hbm, noise, noise_sem, level).wait()
        fetch(diag_hbm, diag, diag_sem, level).wait()
        if level > 0:
            fetch(coup_hbm, coup, coup_sem, level - 1).wait()

    loaded(0)
    own_rows(0, (0, 1))
    pl.semaphore_wait(barrier, n - 1 + m - 1)
    for o in range(1, n):
        need_copy(o).start()
    for o in range(1, n):
        need_copy(o).wait()
    copy = pltpu.make_async_copy(want_v, want, want_sem)
    copy.start()
    copy.wait()
    for h in range(2):
        for o in range(1, n):
            block = own[0, want[n - o, 0, 0]]
            send[0, h, o] = block[h * half : (h + 1) * half]
            block_copy(0, h, o).start()
    keep_own(0)
    write_out(0).start()

    for level in range(1, levels):
        loaded(level)
    for level in range(1, levels - 1):
        for h in range(2):
            receive(level - 1, h)
            for first in range(1, n, GROUP):
                group = range(first, min(first + GROUP, n))
                for o in group:
                    send[level, h, o] = solve(level, want[n - o, level, 0], (h,))
                for o in group:
                    block_copy(level, h, o).start()
        own_rows(level, (0, 1))
        keep_own(level)
        write_out(level).start()

    last = levels - 1
    for h in range(2):
        receive(last - 1, h)
        own_rows(last, (h,))
    write_out(last).start()

    def var_copy(o):
        return pltpu.make_async_remote_copy(
            src_ref=sums,
            dst_ref=vrecv.at[o],
            send_sem=vsend_sem.at[o],
            recv_sem=vrecv_sem.at[o],
            device_id={"samp": lax.rem(q + o, m)},
            device_id_type=MESH,
        )

    for o in range(1, m):
        var_copy(o).start()
    vrecv[0] = sums[...]
    for o in range(1, m):
        var_copy(o).wait()
    total = vrecv[q]
    for j in range(1, m):
        total = total + vrecv[lax.rem(q - j + m, m)]
    var_ref[...] = total * (1.0 / (samp * m))
    for level in range(levels):
        write_out(level).wait()


def body(n, m, noise, diag, coupling, pattern):
    levels, slot_dev, samp, b = noise.shape
    fan = coupling.shape[2]
    lead = -(-levels // 8) * 8
    any_spec = pl.BlockSpec(memory_space=pl.ANY)
    vmem_spec = pl.BlockSpec(memory_space=pltpu.VMEM)
    dma = pltpu.SemaphoreType.DMA
    coupling = coupling.reshape(levels - 1, slot_dev, fan * b, b)
    return pl.pallas_call(
        functools.partial(kernel, n, m),
        out_shape=(
            jax.ShapeDtypeStruct(noise.shape, BF16),
            jax.ShapeDtypeStruct((levels, slot_dev, b), F32),
        ),
        in_specs=[pl.BlockSpec(memory_space=pltpu.SMEM), vmem_spec, any_spec, any_spec, any_spec],
        out_specs=(any_spec, vmem_spec),
        scratch_shapes=[
            pltpu.VMEM(noise.shape, BF16),
            pltpu.VMEM(diag.shape, BF16),
            pltpu.VMEM(coupling.shape, BF16),
            pltpu.VMEM(noise.shape, BF16),
            pltpu.VMEM((2, (levels - 1) * n, samp // 2, b), BF16),
            pltpu.VMEM((levels - 1, 2, n, samp // 2, b), BF16),
            pltpu.VMEM((levels - 1, 2, n, samp // 2, b), BF16),
            pltpu.VMEM((n, lead, 128), jnp.int32),
            pltpu.VMEM((n, lead, 128), jnp.int32),
            pltpu.SMEM((n, lead, 128), jnp.int32),
            pltpu.VMEM((levels, slot_dev, b), F32),
            pltpu.VMEM((m, levels, slot_dev, b), F32),
            dma((levels,)),
            dma((levels,)),
            dma((levels - 1,)),
            dma((levels,)),
            dma((levels - 1, 2, n)),
            dma((levels - 1, 2, n)),
            dma((n,)),
            dma((n,)),
            dma,
            dma((m,)),
            dma((m,)),
        ],
        compiler_params=pltpu.CompilerParams(
            collective_id=0, has_side_effects=True, vmem_limit_bytes=56 * 1024 * 1024
        ),
    )(pattern, pattern, noise, diag, coupling)


def solution(mesh):
    placed = (
        P(None, "rows", "samp", None),
        P(None, "rows", None, None),
        P(None, "rows", None, None, None),
        P(None, "rows", None),
    )
    return jax.shard_map(
        functools.partial(body, mesh.shape["rows"], mesh.shape["samp"]),
        mesh=mesh,
        in_specs=placed,
        out_specs=(P(None, "rows", "samp", None), P(None, "rows", None)),
        check_vma=False,
    )
```

```python
import functools

import jax
import jax.numpy as jnp
from jax import lax
from jax.experimental import pallas as pl
from jax.experimental.pallas import tpu as pltpu
from jax.sharding import PartitionSpec as P

MESH = pl.DeviceIdType.MESH
F32 = jnp.float32
BF16 = jnp.bfloat16


GROUP = 4


def kernel(
    n, m, pat_ref, patv_ref, noise_hbm, diag_hbm, coup_hbm,
    samples_hbm, var_ref,
    noise, diag, coup, own, table, send, recv, need, want_v, want, sums, vrecv,
    noise_sem, diag_sem, coup_sem, out_sem, send_sem, recv_sem,
    nsend_sem, nrecv_sem, want_sem, vsend_sem, vrecv_sem,
):
    levels, slot_dev, samp, b = noise.shape
    fan = pat_ref.shape[2]
    me = lax.axis_index("rows")
    q = lax.axis_index("samp")
    half = samp // 2

    def fetch(src, dst, sem, i):
        return pltpu.make_async_copy(src.at[i], dst.at[i], sem.at[i])

    for i in range(levels):
        fetch(noise_hbm, noise, noise_sem, i).start()
        fetch(diag_hbm, diag, diag_sem, i).start()
    for i in range(levels - 1):
        fetch(coup_hbm, coup, coup_sem, i).start()

    barrier = pltpu.get_barrier_semaphore()
    for o in range(1, n):
        pl.semaphore_signal(
            barrier, inc=1, device_id={"rows": lax.rem(me + o, n)}, device_id_type=MESH
        )
    for o in range(1, m):
        pl.semaphore_signal(
            barrier, inc=1, device_id={"samp": lax.rem(q + o, m)}, device_id_type=MESH
        )

    shape = (need.shape[0], need.shape[1], fan)
    dev = lax.broadcasted_iota(jnp.int32, shape, 0)
    lev = lax.broadcasted_iota(jnp.int32, shape, 1)
    key = lev * n + dev
    best = jnp.zeros(shape, jnp.int32)
    for t in range(levels - 1):
        for s in range(slot_dev):
            entry = patv_ref[t, s : s + 1, :].reshape(1, 1, fan)
            holder = lax.div(entry, jnp.int32(slot_dev))
            slot = entry - holder * slot_dev
            best = jnp.maximum(best, jnp.where(holder == key, slot, 0))
    best = jnp.max(best, axis=2, keepdims=True)
    need[...] = jnp.broadcast_to(best, need.shape)
    want_v[0] = need[me]

    def need_copy(o):
        return pltpu.make_async_remote_copy(
            src_ref=need.at[lax.rem(me + o, n)],
            dst_ref=want_v.at[o],
            send_sem=nsend_sem.at[o],
            recv_sem=nrecv_sem.at[o],
            device_id={"rows": lax.rem(me + o, n)},
            device_id_type=MESH,
        )

    def block_copy(level, h, o):
        return pltpu.make_async_remote_copy(
            src_ref=send.at[level, h, o],
            dst_ref=recv.at[level, h, o],
            send_sem=send_sem.at[level, h, o],
            recv_sem=recv_sem.at[level, h, o],
            device_id={"rows": lax.rem(me + o, n)},
            device_id_type=MESH,
        )

    def holder_of(level, s, k):
        return lax.div(pat_ref[level - 1, s, k], jnp.int32(slot_dev))

    def solve(level, s, halves):
        low, count = halves[0] * half, len(halves) * half
        residual = noise[level, s, pl.ds(low, count), :].astype(F32)
        if level > 0:
            total = None
            for k in range(0, fan, 2):
                picked = [
                    jnp.concatenate(
                        [table[h, holder_of(level, s, k + j)] for h in halves], axis=0
                    )
                    for j in range(2)
                ]
                part = jnp.dot(
                    jnp.concatenate(picked, axis=1),
                    coup[level - 1, s, pl.ds(k * b, 2 * b), :],
                    preferred_element_type=F32,
                )
                total = part if total is None else total + part
            residual = residual - total
        return jnp.dot(
            residual.astype(BF16), diag[level, s], preferred_element_type=F32
        ).astype(BF16)

    def own_rows(level, halves):
        low, count = halves[0] * half, len(halves) * half

        def row(s, carry):
            x = solve(level, s, halves)
            own[level, s, pl.ds(low, count), :] = x
            wide = x.astype(F32)
            part = jnp.sum(wide * wide, axis=0, keepdims=True)
            if low > 0:
                part = part + sums[level, pl.ds(s, 1), :]
            sums[level, pl.ds(s, 1), :] = part
            return carry

        lax.fori_loop(0, slot_dev, row, 0, unroll=8)

    def keep_own(level):
        mine = own[level, want[0, level, 0]]
        for h in range(2):
            table[h, level * n + me] = mine[h * half : (h + 1) * half]

    def receive(level, h):
        for o in range(1, n):
            block_copy(level, h, o).wait()
            table[h, level * n + lax.rem(me - o + n, n)] = recv[level, h, o]

    def write_out(level):
        return pltpu.make_async_copy(own.at[level], samples_hbm.at[level], out_sem.at[level])

    def loaded(level):
        fetch(noise_hbm, noise, noise_sem, level).wait()
        fetch(diag_hbm, diag, diag_sem, level).wait()
        if level > 0:
            fetch(coup_hbm, coup, coup_sem, level - 1).wait()

    loaded(0)
    own_rows(0, (0, 1))
    pl.semaphore_wait(barrier, n - 1 + m - 1)
    for o in range(1, n):
        need_copy(o).start()
    for o in range(1, n):
        need_copy(o).wait()
    copy = pltpu.make_async_copy(want_v, want, want_sem)
    copy.start()
    copy.wait()
    for h in range(2):
        for o in range(1, n):
            block = own[0, want[n - o, 0, 0]]
            send[0, h, o] = block[h * half : (h + 1) * half]
            block_copy(0, h, o).start()
    keep_own(0)
    write_out(0).start()

    for level in range(1, levels):
        loaded(level)
    for level in range(1, levels - 1):
        for h in range(2):
            receive(level - 1, h)
            for first in range(1, n, GROUP):
                group = range(first, min(first + GROUP, n))
                for o in group:
                    send[level, h, o] = solve(level, want[n - o, level, 0], (h,))
                for o in group:
                    block_copy(level, h, o).start()
        own_rows(level, (0, 1))
        keep_own(level)
        write_out(level).start()

    last = levels - 1
    for h in range(2):
        receive(last - 1, h)
        own_rows(last, (h,))
    write_out(last).start()

    def var_copy(o):
        return pltpu.make_async_remote_copy(
            src_ref=sums,
            dst_ref=vrecv.at[o],
            send_sem=vsend_sem.at[o],
            recv_sem=vrecv_sem.at[o],
            device_id={"samp": lax.rem(q + o, m)},
            device_id_type=MESH,
        )

    for o in range(1, m):
        var_copy(o).start()
    vrecv[0] = sums[...]
    for o in range(1, m):
        var_copy(o).wait()
    total = vrecv[q]
    for j in range(1, m):
        total = total + vrecv[lax.rem(q - j + m, m)]
    var_ref[...] = total * (1.0 / (samp * m))
    for level in range(levels):
        write_out(level).wait()


def hand_out(x_hbm, v_hbm, y_hbm, w_hbm, x, v, in_sem, out_sem, v_sem):
    levels = x.shape[0]
    reads = [pltpu.make_async_copy(x_hbm.at[i], x.at[i], in_sem.at[i]) for i in range(levels)]
    writes = [pltpu.make_async_copy(x.at[i], y_hbm.at[i], out_sem.at[i]) for i in range(levels)]
    v_read = pltpu.make_async_copy(v_hbm, v, v_sem.at[0])
    v_write = pltpu.make_async_copy(v, w_hbm, v_sem.at[1])
    v_read.start()
    for copy in reads:
        copy.start()
    v_read.wait()
    v_write.start()
    for i in range(levels):
        reads[i].wait()
        writes[i].start()
    v_write.wait()
    for copy in writes:
        copy.wait()


def body(n, m, noise, diag, coupling, pattern):
    levels, slot_dev, samp, b = noise.shape
    fan = coupling.shape[2]
    lead = -(-levels // 8) * 8
    any_spec = pl.BlockSpec(memory_space=pl.ANY)
    vmem_spec = pl.BlockSpec(memory_space=pltpu.VMEM)
    dma = pltpu.SemaphoreType.DMA
    coupling = coupling.reshape(levels - 1, slot_dev, fan * b, b)
    solved = pl.pallas_call(
        functools.partial(kernel, n, m),
        out_shape=(
            jax.ShapeDtypeStruct(noise.shape, BF16),
            jax.ShapeDtypeStruct((levels, slot_dev, b), F32),
        ),
        in_specs=[pl.BlockSpec(memory_space=pltpu.SMEM), vmem_spec, any_spec, any_spec, any_spec],
        out_specs=(any_spec, vmem_spec),
        scratch_shapes=[
            pltpu.VMEM(noise.shape, BF16),
            pltpu.VMEM(diag.shape, BF16),
            pltpu.VMEM(coupling.shape, BF16),
            pltpu.VMEM(noise.shape, BF16),
            pltpu.VMEM((2, (levels - 1) * n, samp // 2, b), BF16),
            pltpu.VMEM((levels - 1, 2, n, samp // 2, b), BF16),
            pltpu.VMEM((levels - 1, 2, n, samp // 2, b), BF16),
            pltpu.VMEM((n, lead, 128), jnp.int32),
            pltpu.VMEM((n, lead, 128), jnp.int32),
            pltpu.SMEM((n, lead, 128), jnp.int32),
            pltpu.VMEM((levels, slot_dev, b), F32),
            pltpu.VMEM((m, levels, slot_dev, b), F32),
            dma((levels,)),
            dma((levels,)),
            dma((levels - 1,)),
            dma((levels,)),
            dma((levels - 1, 2, n)),
            dma((levels - 1, 2, n)),
            dma((n,)),
            dma((n,)),
            dma,
            dma((m,)),
            dma((m,)),
        ],
        compiler_params=pltpu.CompilerParams(
            collective_id=0, has_side_effects=True, vmem_limit_bytes=56 * 1024 * 1024
        ),
    )(pattern, pattern, noise, diag, coupling)
    return pl.pallas_call(
        hand_out,
        out_shape=tuple(jax.ShapeDtypeStruct(a.shape, a.dtype) for a in solved),
        in_specs=[any_spec, any_spec],
        out_specs=(any_spec, any_spec),
        scratch_shapes=[
            pltpu.VMEM(solved[0].shape, BF16),
            pltpu.VMEM(solved[1].shape, F32),
            dma((levels,)),
            dma((levels,)),
            dma((2,)),
        ],
    )(*solved)


def solution(mesh):
    placed = (
        P(None, "rows", "samp", None),
        P(None, "rows", None, None),
        P(None, "rows", None, None, None),
        P(None, "rows", None),
    )
    return jax.shard_map(
        functools.partial(body, mesh.shape["rows"], mesh.shape["samp"]),
        mesh=mesh,
        in_specs=placed,
        out_specs=(P(None, "rows", "samp", None), P(None, "rows", None)),
        check_vma=False,
    )
```
